32 devices in a mesh: dp: 2 (over y), table: 16 (over z, x, core).
Axes of the slice: x: 2, y: 2, z: 4, core: 2. Of those that a mesh axis runs over, the one named last changes fastest.
Arguments:
- gradients: bfloat16 [256, 4096], P(None, ('dp', 'table')), may hold values from -16 to 16
- row_ids: int32 [4096], P(('dp', 'table')), may hold values from 0 to 32767
- table_block: float32 [256, 32768], P('table', 'dp'), may hold values from -6 to 6
- adagrad_state: float32 [32768], P('dp'), may hold values from 0.05 to 2
Outputs:
- new_table: float32 [256, 32768], P('table', 'dp')
- new_state: float32 [32768], P('dp')
The draws below stay inside these ranges and needn't reach their ends.
All inputs are finite; a program needn't handle non-finite values.
Results may differ from the reference program's by a relative error of at most 0.0003.
Values may be sent and summed in bfloat16 or wider, within the bound.
A program may use at most 64 MiB of HBM per device.

```python
import math
import jax
import jax.numpy as jnp
from jax import lax

W = 256
TILE = 128
ROWS = 32768
LOOKUPS = 4096
TILES = 256


def draw_gradients(key, part):
    first, second = jax.random.split(key, 2)
    rising = 3.0 ** (jnp.arange(W, dtype=jnp.float32) / (W - 1))
    jitter = jnp.exp(jax.random.uniform(second, (W,), jnp.float32, 0.0, math.log(4.0)))
    column = 0.4 * rising * jitter
    values = jax.random.normal(first, (W, LOOKUPS), jnp.float32) * column[:, None]
    return jnp.clip(values, -16.0, 16.0).astype(jnp.bfloat16)


def draw_row_ids(key, part):
    first, second, third = jax.random.split(key, 3)
    heat = jax.random.randint(first, (TILES,), 0, 4)
    weight = jnp.where(heat == 0, 4, 1).astype(jnp.int32)
    cumulative = jnp.cumsum(weight)
    picked = jax.random.randint(second, (LOOKUPS,), 0, cumulative[-1])
    tile_index = jnp.searchsorted(cumulative, picked, side='right').astype(jnp.int32)
    offset = jax.random.randint(third, (LOOKUPS,), 0, TILE)
    result = tile_index * TILE + offset
    result = result.at[0].set(0).at[1].set(ROWS - 1)
    return result.astype(jnp.int32)


def level_of(stream_key, shape, pieces, smallest, largest):
    loudness, own = 1.0, jax.random.fold_in(stream_key, 6)
    for dim, parts in pieces:
        draws = jnp.exp(jax.random.uniform(jax.random.fold_in(own, dim), (parts,), jnp.float32, smallest / len(pieces), largest / len(pieces)))
        loudness = loudness * jnp.repeat(draws, shape[dim] // parts).reshape([-1 if axis == dim else 1 for axis in range(len(shape))])
    return loudness


def gaussian(stream_key, dims, spread, limit, shards=(), kind=jnp.bfloat16):
    level = level_of(stream_key, dims, shards, -0.22, 0.18) if shards else 1.0
    values = jax.random.normal(stream_key, dims, jnp.float32) * spread * level
    return jnp.minimum(jnp.maximum(values, -limit), limit).astype(kind)


def setup_inputs(seed: int = 0) -> dict:
    key_of = jax.random.split(jax.random.key(seed), 5)
    return {
        "gradients": draw_gradients(jax.random.fold_in(key_of[4], 71), 0),
        "row_ids": draw_row_ids(jax.random.fold_in(key_of[4], 71), 0),
        "table_block": gaussian(key_of[2], (W, ROWS), 1.0, 6.0, ((0, 16), (1, 2)), jnp.float32),
        "adagrad_state": jnp.clip(jnp.exp(math.log(2.0) - 3.6888794 * jax.random.uniform(key_of[3], (ROWS,), jnp.float32) ** level_of(key_of[3], (ROWS,), ((0, 2),), -0.2, 0.2)), 0.05, 2.0),
    }


learn_rate = 0.5

def reference(gradients, row_ids, table_block, adagrad_state):
    zeros = jnp.zeros((W, ROWS), jnp.float32)
    row_grad = zeros.at[:, row_ids].add(gradients.astype(jnp.float32))
    new_state = adagrad_state + lax.optimization_barrier(jnp.sum(row_grad * row_grad, axis=0)) / W
    new_table = table_block - learn_rate * row_grad / jnp.sqrt(new_state)[None, :]
    return (new_table, new_state)
```

```python
import functools

import jax
import jax.numpy as jnp
from jax import lax
from jax.experimental import pallas as pl
from jax.experimental.pallas import tpu as pltpu
from jax.sharding import PartitionSpec as P

learn_rate = 0.5
LO = 256
LANES = 128
GROUP = 4
READY = 2
PIECES = 4
MESH = pl.DeviceIdType.MESH


def accumulate(grads, ids, first_row, count_rows):
    relative = ids - first_row
    inside = (relative >= 0) & (relative < count_rows)
    target = jnp.where(inside, relative, count_rows)
    start_total = jnp.zeros((grads.shape[0], count_rows), jnp.float32)
    return start_total.at[:, target].add(grads.astype(jnp.float32), mode="drop")


def plain_body(width, gradients, row_ids, table_block, adagrad_state):
    owned = lax.all_to_all(gradients, "table", split_axis=0, concat_axis=1, tiled=True)
    local_rows = table_block.shape[1]
    all_row_ids = lax.all_gather(row_ids, ("dp", "table"), axis=0, tiled=True)
    first_row = lax.axis_index("dp") * local_rows
    row_grad = accumulate(
        lax.all_gather(owned, "dp", axis=1, tiled=True), all_row_ids, first_row, local_rows
    )
    partial_squares = jnp.sum(row_grad * row_grad, axis=0)
    squares = lax.psum(partial_squares, "table")
    new_state = adagrad_state + squares / width
    new_table = table_block - learn_rate * row_grad / jnp.sqrt(new_state)[None, :]
    return (new_table, new_state)


def flips(value, size):
    table, bit = [value], 1
    while bit < size:
        change = bit - 2 * bit * lax.rem(value // bit, 2)
        table = table + [old + change for old in table]
        bit *= 2
    return table


def ready_groups(chips):
    groups, first = [], 1
    while first < chips:
        size = min(first, READY)
        groups.append(range(first, first + size))
        first += size
    return groups


def exchange_kernel(
    dp, tb, cols, rows, width,
    g_ref, id_ref, state_ref, table_ref, table_out, state_out,
    acc, pair_g, pair_i, got_g, got_i, table, part, red, total, full, state,
    send_g, send_i, send_r, send_a, recv_g, recv_i, recv_r, recv_a, own_sem, ready,
):
    d, t = lax.axis_index("dp"), lax.axis_index("table")
    chips = dp * tb // 2
    his = rows // LO
    lines = rows // tb // LANES
    parts = LO // LANES
    each = his // tb
    first_row = d * rows
    ts, ds = flips(t, tb), flips(d, dp)
    core, spot = lax.rem(t, 2), t // 2
    order = t // 4 * (2 * dp) + d * 2 + lax.rem(spot, 2)
    groups = ready_groups(chips)
    sibling = (d, ts[1])

    def device(m):
        return ds[m // 2 % dp], ts[m % 2 * 2 + m // (2 * dp) * 4]

    def earlier(group):
        top = 1
        while top * 2 <= group[0]:
            top *= 2
        return lax.rem(order // top, 2) == 1

    def signal(semaphore, to):
        pl.semaphore_signal(semaphore, inc=1, device_id=to, device_id_type=MESH)

    def wait_blocks(ref, sem, count):
        there = ref.at[pl.ds(0, count)]
        pltpu.make_async_copy(there, there, sem).wait()

    barrier = pltpu.get_barrier_semaphore()

    @pl.when(core == 0)
    def _():
        signal(barrier, sibling)

    for group in reversed(groups):
        @pl.when(jnp.logical_not(earlier(group)))
        def _(group=group):
            for m in group:
                signal(barrier, device(m))

    own = (
        pltpu.make_async_copy(g_ref.at[:, core], pair_g.at[:, core], own_sem.at[0]),
        pltpu.make_async_copy(id_ref, pair_i.at[core], own_sem.at[1]),
        pltpu.make_async_copy(state_ref, state, own_sem.at[2]),
        pltpu.make_async_copy(table_ref, table, own_sem.at[3]),
    )
    own[0].start()
    own[1].start()

    @pl.when(order + core > 0)
    def _():
        pl.semaphore_wait(barrier, order + core)

    @pl.when(core == 1)
    def _():
        signal(ready.at[0], sibling)

    for g, group in reversed(list(enumerate(groups))):
        @pl.when(earlier(group))
        def _(g=g, group=group):
            for m in group:
                signal(ready.at[g + 1], device(m))

    @pl.when(core == 0)
    def _():
        pl.semaphore_wait(ready.at[0], 1)

    pltpu.make_async_remote_copy(
        src_ref=id_ref, dst_ref=pair_i.at[core],
        send_sem=send_i.at[0], recv_sem=recv_i.at[0],
        device_id=sibling, device_id_type=MESH,
    ).start()
    pltpu.make_async_remote_copy(
        src_ref=g_ref.at[:, 1 - core], dst_ref=pair_g.at[:, core],
        send_sem=send_g.at[0], recv_sem=recv_g.at[0],
        device_id=sibling, device_id_type=MESH,
    ).start()
    own[2].start()
    own[3].start()
    own[0].wait()
    own[1].wait()
    pltpu.make_async_copy(id_ref, pair_i.at[1 - core], recv_i.at[0]).wait()
    pltpu.make_async_copy(g_ref.at[:, 0], pair_g.at[:, 1 - core], recv_g.at[0]).wait()

    def send(m):
        to = device(m)
        pltpu.make_async_remote_copy(
            src_ref=pair_i, dst_ref=got_i.at[m],
            send_sem=send_i.at[1], recv_sem=recv_i.at[1 + m // GROUP],
            device_id=to, device_id_type=MESH,
        ).start()
        pltpu.make_async_remote_copy(
            src_ref=pair_g.at[to[1] // 2], dst_ref=got_g.at[m],
            send_sem=send_g.at[1], recv_sem=recv_g.at[1 + m // GROUP],
            device_id=to, device_id_type=MESH,
        ).start()

    for group in reversed(groups):
        @pl.when(earlier(group))
        def _(group=group):
            for m in reversed(group):
                send(m)

    acc[...] = jnp.zeros_like(acc)
    got_g[0] = pair_g[spot]
    got_i[0] = pair_i[...]

    for g, group in enumerate(groups):
        @pl.when(jnp.logical_not(earlier(group)))
        def _(g=g, group=group):
            pl.semaphore_wait(ready.at[g + 1], len(group))
            for m in group:
                send(m)

    def add(sources):
        both = [(m, c) for m in sources for c in range(2)]
        ids = jnp.concatenate([got_i[m, c] for m, c in both], axis=1) - first_row
        grads = jnp.concatenate([got_g[m, c] for m, c in both], axis=1)
        span = ids.shape[1]
        low = jnp.broadcast_to(lax.bitwise_and(ids, LO - 1), (LO, span))
        place = lax.broadcasted_iota(jnp.int32, (LO, span), 0)
        one_hot = jnp.where(low == place, 1.0, 0.0).astype(jnp.bfloat16)
        high = jnp.broadcast_to(lax.shift_right_arithmetic(ids, 8), (cols, span))
        high = jnp.clip(high, -1, his).astype(jnp.float32).astype(jnp.bfloat16)
        zero = jnp.zeros_like(grads)
        picked = jnp.concatenate(
            [jnp.where(high == jnp.bfloat16(h), grads, zero) for h in range(his)], axis=0
        )
        acc[...] += lax.dot_general(
            picked, one_hot, (((1,), (1,)), ((), ())), preferred_element_type=jnp.float32
        )

    for first in range(0, chips, GROUP):
        count = GROUP if first else GROUP - 1
        wait_blocks(got_i, recv_i.at[1 + first // GROUP], count)
        wait_blocks(got_g, recv_g.at[1 + first // GROUP], count)
        add(range(first, first + GROUP))

    for j in range(tb):
        pieces = []
        for h in range(each):
            at = (j * each + h) * cols
            piece = acc[at:at + cols, :]
            sums = jnp.sum(piece * piece, axis=0, keepdims=True)
            for half in range(parts):
                pieces.append(sums[:, half * LANES:(half + 1) * LANES])
        part[j] = jnp.concatenate(pieces, axis=0)

    for k in reversed(range(1, tb)):
        pltpu.make_async_remote_copy(
            src_ref=part.at[ts[k]], dst_ref=red.at[k],
            send_sem=send_r.at[0], recv_sem=recv_r.at[0],
            device_id=(d, ts[k]), device_id_type=MESH,
        ).start()
    red[0] = part[t]

    own[2].wait()
    own[3].wait()

    wait_blocks(red, recv_r.at[0], tb - 1)
    here = pl.ds(pl.multiple_of(t * lines, lines), lines)
    fresh = state[here, :] + jnp.sum(red[...], axis=0) / width
    total[...] = fresh
    full[t] = fresh
    for k in reversed(range(1, tb)):
        pltpu.make_async_remote_copy(
            src_ref=total, dst_ref=full.at[t],
            send_sem=send_a.at[0], recv_sem=recv_a.at[k // 4],
            device_id=(d, ts[k]), device_id_type=MESH,
        ).start()

    def update(j):
        fresh = full[j]
        state_out[j] = fresh
        scale = learn_rate / jnp.sqrt(fresh)
        for r in range(lines):
            h, half = r // parts, r % parts
            at = pl.multiple_of((j * each + h) * cols, cols)
            lanes = pl.ds(pl.multiple_of((j * lines + r) * LANES, LANES), LANES)
            step = acc[pl.ds(at, cols), half * LANES:(half + 1) * LANES]
            table_out[:, lanes] = table[:, lanes] - step * scale[r:r + 1, :]

    update(t)
    pltpu.make_async_copy(g_ref.at[:, 0], pair_g.at[:, 0], send_g.at[0]).wait()
    pltpu.make_async_copy(id_ref, pair_i.at[0], send_i.at[0]).wait()
    wait_blocks(got_g, send_g.at[1], chips - 1)
    wait_blocks(got_i, send_i.at[1], chips - 1)
    wait_blocks(red, send_r.at[0], tb - 1)
    for first in range(0, tb, 4):
        wait_blocks(full, recv_a.at[first // 4], 4 if first else 3)
        for k in range(max(first, 1), first + 4):
            update(ts[k])
    wait_blocks(full, send_a.at[0], tb - 1)


def finish_kernel(table_ref, state_ref, table_out, state_out, sems):
    rows = table_ref.shape[1]
    size = rows // PIECES
    copies = [
        pltpu.make_async_copy(
            table_ref.at[:, pl.ds(p * size, size)], table_out.at[:, pl.ds(p * size, size)], sems.at[p]
        )
        for p in range(PIECES)
    ]
    copies.append(pltpu.make_async_copy(state_ref, state_out, sems.at[PIECES]))
    for copy in copies:
        copy.start()
    for copy in copies:
        copy.wait()


def kernel_body(dp, tb, width, gradients, row_ids, table_block, adagrad_state):
    cols, rows = table_block.shape
    count = row_ids.shape[0]
    chips = dp * tb // 2
    his = rows // LO
    lines = rows // tb // LANES
    dma = pltpu.SemaphoreType.DMA
    new_table, new_state = pl.pallas_call(
        functools.partial(exchange_kernel, dp, tb, cols, rows, width),
        name="exchange",
        out_shape=(
            pltpu.VMEM((cols, rows), jnp.float32),
            pltpu.VMEM((tb, lines, LANES), jnp.float32),
        ),
        in_specs=[pl.BlockSpec(memory_space=pl.ANY)] * 4,
        out_specs=(pl.BlockSpec(memory_space=pltpu.VMEM),) * 2,
        scratch_shapes=[
            pltpu.VMEM((his * cols, LO), jnp.float32),
            pltpu.VMEM((tb // 2, 2, cols, count), jnp.bfloat16),
            pltpu.VMEM((2, 1, count), jnp.int32),
            pltpu.VMEM((chips, 2, cols, count), jnp.bfloat16),
            pltpu.VMEM((chips, 2, 1, count), jnp.int32),
            pltpu.VMEM((cols, rows), jnp.float32),
            pltpu.VMEM((tb, lines, LANES), jnp.float32),
            pltpu.VMEM((tb, lines, LANES), jnp.float32),
            pltpu.VMEM((lines, LANES), jnp.float32),
            pltpu.VMEM((tb, lines, LANES), jnp.float32),
            pltpu.VMEM((rows // LANES, LANES), jnp.float32),
            dma((2,)), dma((2,)), dma((1,)), dma((1,)),
            dma((1 + chips // GROUP,)), dma((1 + chips // GROUP,)), dma((1,)), dma((tb // 4,)),
            dma((4,)),
            pltpu.SemaphoreType.REGULAR((1 + len(ready_groups(chips)),)),
        ],
        compiler_params=pltpu.CompilerParams(collective_id=0, has_side_effects=True),
    )(
        gradients.reshape(tb // 2, 2, cols, count),
        row_ids.reshape(1, count),
        adagrad_state.reshape(rows // LANES, LANES),
        table_block,
    )
    new_table, new_state = pl.pallas_call(
        finish_kernel,
        name="finish",
        out_shape=(
            jax.ShapeDtypeStruct((cols, rows), jnp.float32),
            jax.ShapeDtypeStruct((tb, lines, LANES), jnp.float32),
        ),
        in_specs=[pl.BlockSpec(memory_space=pltpu.VMEM)] * 2,
        out_specs=(pl.BlockSpec(memory_space=pl.ANY),) * 2,
        scratch_shapes=[dma((PIECES + 1,))],
    )(
        pltpu.with_memory_space_constraint(new_table, pltpu.VMEM),
        pltpu.with_memory_space_constraint(new_state, pltpu.VMEM),
    )
    return (new_table, new_state.reshape(rows))


def body(dp, tb, gradients, row_ids, table_block, adagrad_state):
    width = gradients.shape[0]
    cols, rows = table_block.shape
    fits = (
        cols % 16 == 0
        and rows % (tb * 8 * LANES) == 0
        and rows % (4 * LO * 4) == 0
        and dp & (dp - 1) == 0
        and tb & (tb - 1) == 0
        and tb % 4 == 0
        and dp * tb % (2 * GROUP) == 0
        and rows // LO <= 256
        and row_ids.shape[0] == LANES
    )
    args = (gradients, row_ids, table_block, adagrad_state)
    if fits:
        return kernel_body(dp, tb, width, *args)
    return plain_body(width, *args)


def solution(mesh):
    in_specs = (P(None, ("dp", "table")), P(("dp", "table")), P("table", "dp"), P("dp"))
    out_specs = (P("table", "dp"), P("dp"))
    run = functools.partial(body, mesh.shape["dp"], mesh.shape["table"])
    return jax.shard_map(run, mesh=mesh, in_specs=in_specs, out_specs=out_specs, check_vma=False)
```

```python
import functools

import jax
import jax.numpy as jnp
from jax import lax
from jax.experimental import pallas as pl
from jax.experimental.pallas import tpu as pltpu
from jax.sharding import PartitionSpec as P

learn_rate = 0.5
LO = 256
LANES = 128
GROUP = 4
READY = 2
PIECES = 2
MESH = pl.DeviceIdType.MESH


def accumulate(grads, ids, first_row, count_rows):
    relative = ids - first_row
    inside = (relative >= 0) & (relative < count_rows)
    target = jnp.where(inside, relative, count_rows)
    start_total = jnp.zeros((grads.shape[0], count_rows), jnp.float32)
    return start_total.at[:, target].add(grads.astype(jnp.float32), mode="drop")


def plain_body(width, gradients, row_ids, table_block, adagrad_state):
    owned = lax.all_to_all(gradients, "table", split_axis=0, concat_axis=1, tiled=True)
    local_rows = table_block.shape[1]
    all_row_ids = lax.all_gather(row_ids, ("dp", "table"), axis=0, tiled=True)
    first_row = lax.axis_index("dp") * local_rows
    row_grad = accumulate(
        lax.all_gather(owned, "dp", axis=1, tiled=True), all_row_ids, first_row, local_rows
    )
    partial_squares = jnp.sum(row_grad * row_grad, axis=0)
    squares = lax.psum(partial_squares, "table")
    new_state = adagrad_state + squares / width
    new_table = table_block - learn_rate * row_grad / jnp.sqrt(new_state)[None, :]
    return (new_table, new_state)


def flips(value, size):
    table, bit = [value], 1
    while bit < size:
        change = bit - 2 * bit * lax.rem(value // bit, 2)
        table = table + [old + change for old in table]
        bit *= 2
    return table


def ready_groups(chips):
    groups, first = [], 1
    while first < chips:
        size = min(first, READY)
        groups.append(range(first, first + size))
        first += size
    return groups


def exchange_kernel(
    dp, tb, cols, rows, width,
    g_ref, id_ref, state_ref, table_ref, table_out, state_out,
    acc, pair_g, pair_i, got_g, got_i, table, part, red, total, full, state,
    send_g, send_i, send_r, send_a, recv_g, recv_i, recv_r, recv_a, own_sem, ready,
):
    d, t = lax.axis_index("dp"), lax.axis_index("table")
    chips = dp * tb // 2
    his = rows // LO
    lines = rows // tb // LANES
    parts = LO // LANES
    each = his // tb
    first_row = d * rows
    ts, ds = flips(t, tb), flips(d, dp)
    core, spot = lax.rem(t, 2), t // 2
    order = t // 4 * (2 * dp) + d * 2 + lax.rem(spot, 2)
    groups = ready_groups(chips)
    sibling = (d, ts[1])

    def device(m):
        return ds[m // 2 % dp], ts[m % 2 * 2 + m // (2 * dp) * 4]

    def earlier(group):
        top = 1
        while top * 2 <= group[0]:
            top *= 2
        return lax.rem(order // top, 2) == 1

    def signal(semaphore, to):
        pl.semaphore_signal(semaphore, inc=1, device_id=to, device_id_type=MESH)

    def wait_blocks(ref, sem, count):
        there = ref.at[pl.ds(0, count)]
        pltpu.make_async_copy(there, there, sem).wait()

    barrier = pltpu.get_barrier_semaphore()

    @pl.when(core == 0)
    def _():
        signal(barrier, sibling)

    for group in reversed(groups):
        @pl.when(jnp.logical_not(earlier(group)))
        def _(group=group):
            for m in group:
                signal(barrier, device(m))

    own = (
        pltpu.make_async_copy(g_ref.at[:, core], pair_g.at[:, core], own_sem.at[0]),
        pltpu.make_async_copy(id_ref, pair_i.at[core], own_sem.at[1]),
        pltpu.make_async_copy(state_ref, state, own_sem.at[2]),
        pltpu.make_async_copy(table_ref, table, own_sem.at[3]),
    )
    own[0].start()
    own[1].start()

    @pl.when(order + core > 0)
    def _():
        pl.semaphore_wait(barrier, order + core)

    @pl.when(core == 1)
    def _():
        signal(ready.at[0], sibling)

    for g, group in reversed(list(enumerate(groups))):
        @pl.when(earlier(group))
        def _(g=g, group=group):
            for m in group:
                signal(ready.at[g + 1], device(m))

    @pl.when(core == 0)
    def _():
        pl.semaphore_wait(ready.at[0], 1)

    pltpu.make_async_remote_copy(
        src_ref=id_ref, dst_ref=pair_i.at[core],
        send_sem=send_i.at[0], recv_sem=recv_i.at[0],
        device_id=sibling, device_id_type=MESH,
    ).start()
    pltpu.make_async_remote_copy(
        src_ref=g_ref.at[:, 1 - core], dst_ref=pair_g.at[:, core],
        send_sem=send_g.at[0], recv_sem=recv_g.at[0],
        device_id=sibling, device_id_type=MESH,
    ).start()
    own[2].start()
    own[3].start()
    own[0].wait()
    own[1].wait()
    pltpu.make_async_copy(id_ref, pair_i.at[1 - core], recv_i.at[0]).wait()
    pltpu.make_async_copy(g_ref.at[:, 0], pair_g.at[:, 1 - core], recv_g.at[0]).wait()

    def send(m):
        to = device(m)
        pltpu.make_async_remote_copy(
            src_ref=pair_i, dst_ref=got_i.at[m],
            send_sem=send_i.at[1], recv_sem=recv_i.at[1 + m // GROUP],
            device_id=to, device_id_type=MESH,
        ).start()
        pltpu.make_async_remote_copy(
            src_ref=pair_g.at[to[1] // 2], dst_ref=got_g.at[m],
            send_sem=send_g.at[1], recv_sem=recv_g.at[1 + m // GROUP],
            device_id=to, device_id_type=MESH,
        ).start()

    for group in reversed(groups):
        @pl.when(earlier(group))
        def _(group=group):
            for m in reversed(group):
                send(m)

    acc[...] = jnp.zeros_like(acc)
    pltpu.make_async_copy(pair_g.at[spot], got_g.at[0], recv_g.at[1]).start()
    pltpu.make_async_copy(pair_i, got_i.at[0], recv_i.at[1]).start()

    for g, group in enumerate(groups):
        @pl.when(jnp.logical_not(earlier(group)))
        def _(g=g, group=group):
            pl.semaphore_wait(ready.at[g + 1], len(group))
            for m in group:
                send(m)

    def add(sources):
        both = [(m, c) for m in sources for c in range(2)]
        ids = jnp.concatenate([got_i[m, c] for m, c in both], axis=1) - first_row
        grads = jnp.concatenate([got_g[m, c] for m, c in both], axis=1)
        span = ids.shape[1]
        low = jnp.broadcast_to(lax.bitwise_and(ids, LO - 1), (LO, span))
        place = lax.broadcasted_iota(jnp.int32, (LO, span), 0)
        one_hot = jnp.where(low == place, 1.0, 0.0).astype(jnp.bfloat16)
        high = jnp.broadcast_to(lax.shift_right_arithmetic(ids, 8), (cols, span))
        high = jnp.clip(high, -1, his).astype(jnp.float32).astype(jnp.bfloat16)
        zero = jnp.zeros_like(grads)
        picked = jnp.concatenate(
            [jnp.where(high == jnp.bfloat16(h), grads, zero) for h in range(his)], axis=0
        )
        acc[...] += lax.dot_general(
            picked, one_hot, (((1,), (1,)), ((), ())), preferred_element_type=jnp.float32
        )

    @pl.loop(0, chips // GROUP)
    def _(g):
        wait_blocks(got_i, recv_i.at[1 + g], GROUP)
        wait_blocks(got_g, recv_g.at[1 + g], GROUP)
        add([g * GROUP + m for m in range(GROUP)])

    for j in range(tb):
        pieces = []
        for h in range(each):
            at = (j * each + h) * cols
            piece = acc[at:at + cols, :]
            sums = jnp.sum(piece * piece, axis=0, keepdims=True)
            for half in range(parts):
                pieces.append(sums[:, half * LANES:(half + 1) * LANES])
        part[j] = jnp.concatenate(pieces, axis=0)

    for k in reversed(range(1, tb)):
        pltpu.make_async_remote_copy(
            src_ref=part.at[ts[k]], dst_ref=red.at[k],
            send_sem=send_r.at[0], recv_sem=recv_r.at[0],
            device_id=(d, ts[k]), device_id_type=MESH,
        ).start()
    red[0] = part[t]

    own[2].wait()
    own[3].wait()

    wait_blocks(red, recv_r.at[0], tb - 1)
    here = pl.ds(pl.multiple_of(t * lines, lines), lines)
    fresh = state[here, :] + jnp.sum(red[...], axis=0) / width
    total[...] = fresh
    full[t] = fresh
    for k in reversed(range(1, tb)):
        pltpu.make_async_remote_copy(
            src_ref=total, dst_ref=full.at[t],
            send_sem=send_a.at[0], recv_sem=recv_a.at[k // 4],
            device_id=(d, ts[k]), device_id_type=MESH,
        ).start()

    def update(j):
        fresh = full[j]
        state_out[j] = fresh
        scale = learn_rate / jnp.sqrt(fresh)
        for r in range(lines):
            h, half = r // parts, r % parts
            at = pl.multiple_of((j * each + h) * cols, cols)
            lanes = pl.ds(pl.multiple_of((j * lines + r) * LANES, LANES), LANES)
            step = acc[pl.ds(at, cols), half * LANES:(half + 1) * LANES]
            table_out[:, lanes] = table[:, lanes] - step * scale[r:r + 1, :]

    update(t)
    pltpu.make_async_copy(g_ref.at[:, 0], pair_g.at[:, 0], send_g.at[0]).wait()
    pltpu.make_async_copy(id_ref, pair_i.at[0], send_i.at[0]).wait()
    wait_blocks(got_g, send_g.at[1], chips - 1)
    wait_blocks(got_i, send_i.at[1], chips - 1)
    wait_blocks(red, send_r.at[0], tb - 1)
    for first in range(0, tb, 4):
        wait_blocks(full, recv_a.at[first // 4], 4 if first else 3)
        for k in range(max(first, 1), first + 4):
            update(ts[k])
    wait_blocks(full, send_a.at[0], tb - 1)


def finish_kernel(table_ref, state_ref, table_out, state_out, sems):
    rows = table_ref.shape[1]
    size = rows // PIECES
    copies = [
        pltpu.make_async_copy(
            table_ref.at[:, pl.ds(p * size, size)], table_out.at[:, pl.ds(p * size, size)], sems.at[p]
        )
        for p in range(PIECES)
    ]
    copies.append(pltpu.make_async_copy(state_ref, state_out, sems.at[PIECES]))
    for copy in copies:
        copy.start()
    for copy in copies:
        copy.wait()


def kernel_body(dp, tb, width, gradients, row_ids, table_block, adagrad_state):
    cols, rows = table_block.shape
    count = row_ids.shape[0]
    chips = dp * tb // 2
    his = rows // LO
    lines = rows // tb // LANES
    dma = pltpu.SemaphoreType.DMA
    new_table, new_state = pl.pallas_call(
        functools.partial(exchange_kernel, dp, tb, cols, rows, width),
        name="exchange",
        out_shape=(
            pltpu.VMEM((cols, rows), jnp.float32),
            pltpu.VMEM((tb, lines, LANES), jnp.float32),
        ),
        in_specs=[pl.BlockSpec(memory_space=pl.ANY)] * 4,
        out_specs=(pl.BlockSpec(memory_space=pltpu.VMEM),) * 2,
        scratch_shapes=[
            pltpu.VMEM((his * cols, LO), jnp.float32),
            pltpu.VMEM((tb // 2, 2, cols, count), jnp.bfloat16),
            pltpu.VMEM((2, 1, count), jnp.int32),
            pltpu.VMEM((chips, 2, cols, count), jnp.bfloat16),
            pltpu.VMEM((chips, 2, 1, count), jnp.int32),
            pltpu.VMEM((cols, rows), jnp.float32),
            pltpu.VMEM((tb, lines, LANES), jnp.float32),
            pltpu.VMEM((tb, lines, LANES), jnp.float32),
            pltpu.VMEM((lines, LANES), jnp.float32),
            pltpu.VMEM((tb, lines, LANES), jnp.float32),
            pltpu.VMEM((rows // LANES, LANES), jnp.float32),
            dma((2,)), dma((2,)), dma((1,)), dma((1,)),
            dma((1 + chips // GROUP,)), dma((1 + chips // GROUP,)), dma((1,)), dma((tb // 4,)),
            dma((4,)),
            pltpu.SemaphoreType.REGULAR((1 + len(ready_groups(chips)),)),
        ],
        compiler_params=pltpu.CompilerParams(collective_id=0, has_side_effects=True),
    )(
        gradients.reshape(tb // 2, 2, cols, count),
        row_ids.reshape(1, count),
        adagrad_state.reshape(rows // LANES, LANES),
        table_block,
    )
    new_table, new_state = pl.pallas_call(
        finish_kernel,
        name="finish",
        out_shape=(
            jax.ShapeDtypeStruct((cols, rows), jnp.float32),
            jax.ShapeDtypeStruct((tb, lines, LANES), jnp.float32),
        ),
        in_specs=[pl.BlockSpec(memory_space=pltpu.VMEM)] * 2,
        out_specs=(pl.BlockSpec(memory_space=pl.ANY),) * 2,
        scratch_shapes=[dma((PIECES + 1,))],
    )(
        pltpu.with_memory_space_constraint(new_table, pltpu.VMEM),
        pltpu.with_memory_space_constraint(new_state, pltpu.VMEM),
    )
    return (new_table, new_state.reshape(rows))


def body(dp, tb, gradients, row_ids, table_block, adagrad_state):
    width = gradients.shape[0]
    cols, rows = table_block.shape
    fits = (
        cols % 16 == 0
        and rows % (tb * 8 * LANES) == 0
        and rows % (4 * LO * 4) == 0
        and dp & (dp - 1) == 0
        and tb & (tb - 1) == 0
        and tb % 4 == 0
        and dp * tb % (2 * GROUP) == 0
        and rows // LO <= 256
        and row_ids.shape[0] == LANES
    )
    args = (gradients, row_ids, table_block, adagrad_state)
    if fits:
        return kernel_body(dp, tb, width, *args)
    return plain_body(width, *args)


def solution(mesh):
    in_specs = (P(None, ("dp", "table")), P(("dp", "table")), P("table", "dp"), P("dp"))
    out_specs = (P("table", "dp"), P("dp"))
    run = functools.partial(body, mesh.shape["dp"], mesh.shape["table"])
    return jax.shard_map(run, mesh=mesh, in_specs=in_specs, out_specs=out_specs, check_vma=False)
```

```python
import functools

import jax
import jax.numpy as jnp
from jax import lax
from jax.experimental import pallas as pl
from jax.experimental.pallas import tpu as pltpu
from jax.sharding import PartitionSpec as P

learn_rate = 0.5
LO = 256
LANES = 128
GROUP = 4
READY = 2
PIECES = 4
MESH = pl.DeviceIdType.MESH


def accumulate(grads, ids, first_row, count_rows):
    relative = ids - first_row
    inside = (relative >= 0) & (relative < count_rows)
    target = jnp.where(inside, relative, count_rows)
    start_total = jnp.zeros((grads.shape[0], count_rows), jnp.float32)
    return start_total.at[:, target].add(grads.astype(jnp.float32), mode="drop")


def plain_body(width, gradients, row_ids, table_block, adagrad_state):
    owned = lax.all_to_all(gradients, "table", split_axis=0, concat_axis=1, tiled=True)
    local_rows = table_block.shape[1]
    all_row_ids = lax.all_gather(row_ids, ("dp", "table"), axis=0, tiled=True)
    first_row = lax.axis_index("dp") * local_rows
    row_grad = accumulate(
        lax.all_gather(owned, "dp", axis=1, tiled=True), all_row_ids, first_row, local_rows
    )
    partial_squares = jnp.sum(row_grad * row_grad, axis=0)
    squares = lax.psum(partial_squares, "table")
    new_state = adagrad_state + squares / width
    new_table = table_block - learn_rate * row_grad / jnp.sqrt(new_state)[None, :]
    return (new_table, new_state)


def flips(value, size):
    table, bit = [value], 1
    while bit < size:
        change = bit - 2 * bit * lax.rem(value // bit, 2)
        table = table + [old + change for old in table]
        bit *= 2
    return table


def ready_groups(chips):
    groups, first = [], 1
    while first < chips:
        size = min(first, READY)
        groups.append(range(first, first + size))
        first += size
    return groups


def exchange_kernel(
    dp, tb, cols, rows, width,
    g_ref, id_ref, state_ref, table_ref, acc, table, state_out,
    pair_g, pair_i, got_g, got_i, part, red, total, full, state,
    send_g, send_i, send_r, send_a, recv_g, recv_i, recv_r, recv_a, own_sem, ready,
):
    d, t = lax.axis_index("dp"), lax.axis_index("table")
    chips = dp * tb // 2
    his = rows // LO
    lines = rows // tb // LANES
    parts = LO // LANES
    each = his // tb
    first_row = d * rows
    ts, ds = flips(t, tb), flips(d, dp)
    core, spot = lax.rem(t, 2), t // 2
    order = t // 4 * (2 * dp) + d * 2 + lax.rem(spot, 2)
    groups = ready_groups(chips)
    sibling = (d, ts[1])
    middle = lax.rem(t // 4 + t // 8, 2) == 1
    far = chips * 3 // 4

    def turns(sequence, near_first):
        sequence = list(sequence)
        close = [group for group in sequence if group[0] < chips // 2]
        cross = [group for group in sequence if chips // 2 <= group[0] < far]
        long = [group for group in sequence if far <= group[0]]
        if near_first:
            first = [(True, group) for group in close]
            return first + [(middle, group) for group in long] + [(True, group) for group in cross] + [
                (jnp.logical_not(middle), group) for group in long
            ]
        last = [(True, group) for group in close]
        return [(middle, group) for group in cross] + [(True, group) for group in long] + [
            (jnp.logical_not(middle), group) for group in cross
        ] + last

    def device(m):
        return ds[m // 2 % dp], ts[m % 2 * 2 + m // (2 * dp) * 4]

    def earlier(group):
        top = 1
        while top * 2 <= group[0]:
            top *= 2
        return lax.rem(order // top, 2) == 1

    def signal(semaphore, to):
        pl.semaphore_signal(semaphore, inc=1, device_id=to, device_id_type=MESH)

    def wait_blocks(ref, sem, count):
        there = ref.at[pl.ds(0, count)]
        pltpu.make_async_copy(there, there, sem).wait()

    barrier = pltpu.get_barrier_semaphore()

    @pl.when(core == 0)
    def _():
        signal(barrier, sibling)

    for group in reversed(groups):
        @pl.when(jnp.logical_not(earlier(group)))
        def _(group=group):
            for m in group:
                signal(barrier, device(m))

    own = (
        pltpu.make_async_copy(g_ref.at[:, core], pair_g.at[:, core], own_sem.at[0]),
        pltpu.make_async_copy(id_ref, pair_i.at[core], own_sem.at[1]),
        pltpu.make_async_copy(state_ref, state, own_sem.at[2]),
        pltpu.make_async_copy(table_ref, table, own_sem.at[3]),
    )
    own[0].start()
    own[1].start()

    @pl.when(order + core > 0)
    def _():
        pl.semaphore_wait(barrier, order + core)

    @pl.when(core == 1)
    def _():
        signal(ready.at[0], sibling)

    for g, group in reversed(list(enumerate(groups))):
        @pl.when(earlier(group))
        def _(g=g, group=group):
            for m in group:
                signal(ready.at[g + 1], device(m))

    @pl.when(core == 0)
    def _():
        pl.semaphore_wait(ready.at[0], 1)

    pltpu.make_async_remote_copy(
        src_ref=id_ref, dst_ref=pair_i.at[core],
        send_sem=send_i.at[0], recv_sem=recv_i.at[0],
        device_id=sibling, device_id_type=MESH,
    ).start()
    pltpu.make_async_remote_copy(
        src_ref=g_ref.at[:, 1 - core], dst_ref=pair_g.at[:, core],
        send_sem=send_g.at[0], recv_sem=recv_g.at[0],
        device_id=sibling, device_id_type=MESH,
    ).start()
    own[2].start()
    own[3].start()
    own[0].wait()
    own[1].wait()
    pltpu.make_async_copy(id_ref, pair_i.at[1 - core], recv_i.at[0]).wait()
    pltpu.make_async_copy(g_ref.at[:, 0], pair_g.at[:, 1 - core], recv_g.at[0]).wait()

    def send(m):
        to = device(m)
        pltpu.make_async_remote_copy(
            src_ref=pair_i, dst_ref=got_i.at[m],
            send_sem=send_i.at[1], recv_sem=recv_i.at[1 + m // GROUP],
            device_id=to, device_id_type=MESH,
        ).start()
        pltpu.make_async_remote_copy(
            src_ref=pair_g.at[to[1] // 2], dst_ref=got_g.at[m],
            send_sem=send_g.at[1], recv_sem=recv_g.at[1 + m // GROUP],
            device_id=to, device_id_type=MESH,
        ).start()

    for turn, group in turns(reversed(groups), False):
        @pl.when(jnp.logical_and(earlier(group), turn))
        def _(group=group):
            for m in reversed(group):
                send(m)

    acc[...] = jnp.zeros_like(acc)
    pltpu.make_async_copy(pair_g.at[spot], got_g.at[0], recv_g.at[1]).start()
    pltpu.make_async_copy(pair_i, got_i.at[0], recv_i.at[1]).start()

    for turn, group in turns(groups, True):
        @pl.when(jnp.logical_and(jnp.logical_not(earlier(group)), turn))
        def _(g=groups.index(group), group=group):
            pl.semaphore_wait(ready.at[g + 1], len(group))
            for m in group:
                send(m)

    def add(sources):
        both = [(m, c) for m in sources for c in range(2)]
        ids = jnp.concatenate([got_i[m, c] for m, c in both], axis=1) - first_row
        grads = jnp.concatenate([got_g[m, c] for m, c in both], axis=1)
        span = ids.shape[1]
        low = jnp.broadcast_to(lax.bitwise_and(ids, LO - 1), (LO, span))
        place = lax.broadcasted_iota(jnp.int32, (LO, span), 0)
        one_hot = jnp.where(low == place, 1.0, 0.0).astype(jnp.bfloat16)
        high = jnp.broadcast_to(lax.shift_right_arithmetic(ids, 8), (cols, span))
        high = jnp.clip(high, -1, his).astype(jnp.float32).astype(jnp.bfloat16)
        zero = jnp.zeros_like(grads)
        picked = jnp.concatenate(
            [jnp.where(high == jnp.bfloat16(h), grads, zero) for h in range(his)], axis=0
        )
        acc[...] += lax.dot_general(
            picked, one_hot, (((1,), (1,)), ((), ())), preferred_element_type=jnp.float32
        )

    @pl.loop(0, chips // GROUP)
    def _(turn):
        half = chips // GROUP // 2
        quarter = chips // GROUP // 4
        swap = jnp.where(jnp.logical_and(middle, turn >= half), 1, 0)
        g = turn + swap * (quarter - 2 * quarter * ((turn - half) // quarter))
        wait_blocks(got_i, recv_i.at[1 + g], GROUP)
        wait_blocks(got_g, recv_g.at[1 + g], GROUP)
        add([g * GROUP + m for m in range(GROUP)])

    def part_copy(k):
        return pltpu.make_async_remote_copy(
            src_ref=part.at[k], dst_ref=red.at[k],
            send_sem=send_r.at[0], recv_sem=recv_r.at[0],
            device_id=(d, ts[k]), device_id_type=MESH,
        )

    for k in reversed(range(tb)):
        pieces = []
        for h in range(each):
            at = pl.multiple_of((ts[k] * each + h) * cols, cols)
            piece = acc[pl.ds(at, cols), :]
            sums = jnp.sum(piece * piece, axis=0, keepdims=True)
            for half in range(parts):
                pieces.append(sums[:, half * LANES:(half + 1) * LANES])
        part[k] = jnp.concatenate(pieces, axis=0)
        if k + 1 < tb:
            part_copy(k + 1).start()
    red[0] = part[0]

    own[2].wait()
    own[3].wait()

    wait_blocks(red, recv_r.at[0], tb - 1)
    here = pl.ds(pl.multiple_of(t * lines, lines), lines)
    fresh = state[here, :] + jnp.sum(red[...], axis=0) / width
    total[...] = fresh
    full[t] = fresh
    for k in reversed(range(1, tb)):
        pltpu.make_async_remote_copy(
            src_ref=total, dst_ref=full.at[t],
            send_sem=send_a.at[0], recv_sem=recv_a.at[0],
            device_id=(d, ts[k]), device_id_type=MESH,
        ).start()

    pltpu.make_async_copy(g_ref.at[:, 0], pair_g.at[:, 0], send_g.at[0]).wait()
    pltpu.make_async_copy(id_ref, pair_i.at[0], send_i.at[0]).wait()
    wait_blocks(got_g, send_g.at[1], chips - 1)
    wait_blocks(got_i, send_i.at[1], chips - 1)
    wait_blocks(red, send_r.at[0], tb - 1)
    wait_blocks(full, recv_a.at[0], tb - 1)
    state_out[...] = full[...]
    wait_blocks(full, send_a.at[0], tb - 1)


def finish_kernel(acc, table, state, table_out, state_out, fresh_table, sems):
    teams, lines, _ = state.shape
    cols, rows = table.shape
    parts = LO // LANES
    each = lines // parts
    size = rows // PIECES
    copies = [pltpu.make_async_copy(state, state_out, sems.at[PIECES])]
    copies[0].start()
    for p in range(PIECES):
        for j in range(p * teams // PIECES, (p + 1) * teams // PIECES):
            scale = learn_rate / jnp.sqrt(state[j])
            for r in range(lines):
                at, half = (j * each + r // parts) * cols, r % parts
                lanes = slice((j * lines + r) * LANES, (j * lines + r + 1) * LANES)
                step = acc[at:at + cols, half * LANES:(half + 1) * LANES]
                fresh_table[:, lanes] = table[:, lanes] - step * scale[r:r + 1, :]
        there = pl.ds(p * size, size)
        copies.append(pltpu.make_async_copy(fresh_table.at[:, there], table_out.at[:, there], sems.at[p]))
        copies[-1].start()
    for copy in copies:
        copy.wait()


def kernel_body(dp, tb, width, gradients, row_ids, table_block, adagrad_state):
    cols, rows = table_block.shape
    count = row_ids.shape[0]
    chips = dp * tb // 2
    his = rows // LO
    lines = rows // tb // LANES
    dma = pltpu.SemaphoreType.DMA
    row_grad, table, state = pl.pallas_call(
        functools.partial(exchange_kernel, dp, tb, cols, rows, width),
        name="exchange",
        out_shape=(
            pltpu.VMEM((his * cols, LO), jnp.float32),
            pltpu.VMEM((cols, rows), jnp.float32),
            pltpu.VMEM((tb, lines, LANES), jnp.float32),
        ),
        in_specs=[pl.BlockSpec(memory_space=pl.ANY)] * 4,
        out_specs=(pl.BlockSpec(memory_space=pltpu.VMEM),) * 3,
        scratch_shapes=[
            pltpu.VMEM((tb // 2, 2, cols, count), jnp.bfloat16),
            pltpu.VMEM((2, 1, count), jnp.int32),
            pltpu.VMEM((chips, 2, cols, count), jnp.bfloat16),
            pltpu.VMEM((chips, 2, 1, count), jnp.int32),
            pltpu.VMEM((tb, lines, LANES), jnp.float32),
            pltpu.VMEM((tb, lines, LANES), jnp.float32),
            pltpu.VMEM((lines, LANES), jnp.float32),
            pltpu.VMEM((tb, lines, LANES), jnp.float32),
            pltpu.VMEM((rows // LANES, LANES), jnp.float32),
            dma((2,)), dma((2,)), dma((1,)), dma((1,)),
            dma((1 + chips // GROUP,)), dma((1 + chips // GROUP,)), dma((1,)), dma((1,)),
            dma((4,)),
            pltpu.SemaphoreType.REGULAR((1 + len(ready_groups(chips)),)),
        ],
        compiler_params=pltpu.CompilerParams(collective_id=0, has_side_effects=True),
    )(
        gradients.reshape(tb // 2, 2, cols, count),
        row_ids.reshape(1, count),
        adagrad_state.reshape(rows // LANES, LANES),
        table_block,
    )
    new_table, new_state = pl.pallas_call(
        finish_kernel,
        name="finish",
        out_shape=(
            jax.ShapeDtypeStruct((cols, rows), jnp.float32),
            jax.ShapeDtypeStruct((tb, lines, LANES), jnp.float32),
        ),
        in_specs=[pl.BlockSpec(memory_space=pltpu.VMEM)] * 3,
        out_specs=(pl.BlockSpec(memory_space=pl.ANY),) * 2,
        scratch_shapes=[pltpu.VMEM((cols, rows), jnp.float32), dma((PIECES + 1,))],
    )(
        pltpu.with_memory_space_constraint(row_grad, pltpu.VMEM),
        pltpu.with_memory_space_constraint(table, pltpu.VMEM),
        pltpu.with_memory_space_constraint(state, pltpu.VMEM),
    )
    return (new_table, new_state.reshape(rows))


def body(dp, tb, gradients, row_ids, table_block, adagrad_state):
    width = gradients.shape[0]
    cols, rows = table_block.shape
    fits = (
        cols % 16 == 0
        and rows % (tb * 8 * LANES) == 0
        and rows % (4 * LO * 4) == 0
        and dp & (dp - 1) == 0
        and tb & (tb - 1) == 0
        and tb % 4 == 0
        and dp * tb % (8 * GROUP) == 0
        and rows // LO <= 256
        and row_ids.shape[0] == LANES
    )
    args = (gradients, row_ids, table_block, adagrad_state)
    if fits:
        return kernel_body(dp, tb, width, *args)
    return plain_body(width, *args)


def solution(mesh):
    in_specs = (P(None, ("dp", "table")), P(("dp", "table")), P("table", "dp"), P("dp"))
    out_specs = (P("table", "dp"), P("dp"))
    run = functools.partial(body, mesh.shape["dp"], mesh.shape["table"])
    return jax.shard_map(run, mesh=mesh, in_specs=in_specs, out_specs=out_specs, check_vma=False)
```

```python
import functools

import jax
import jax.numpy as jnp
from jax import lax
from jax.experimental import pallas as pl
from jax.experimental.pallas import tpu as pltpu
from jax.sharding import PartitionSpec as P

learn_rate = 0.5
LO = 256
LANES = 128
GROUP = 4
READY = 2
PIECES = 4
MESH = pl.DeviceIdType.MESH


def accumulate(grads, ids, first_row, count_rows):
    relative = ids - first_row
    inside = (relative >= 0) & (relative < count_rows)
    target = jnp.where(inside, relative, count_rows)
    start_total = jnp.zeros((grads.shape[0], count_rows), jnp.float32)
    return start_total.at[:, target].add(grads.astype(jnp.float32), mode="drop")


def plain_body(width, gradients, row_ids, table_block, adagrad_state):
    owned = lax.all_to_all(gradients, "table", split_axis=0, concat_axis=1, tiled=True)
    local_rows = table_block.shape[1]
    all_row_ids = lax.all_gather(row_ids, ("dp", "table"), axis=0, tiled=True)
    first_row = lax.axis_index("dp") * local_rows
    row_grad = accumulate(
        lax.all_gather(owned, "dp", axis=1, tiled=True), all_row_ids, first_row, local_rows
    )
    partial_squares = jnp.sum(row_grad * row_grad, axis=0)
    squares = lax.psum(partial_squares, "table")
    new_state = adagrad_state + squares / width
    new_table = table_block - learn_rate * row_grad / jnp.sqrt(new_state)[None, :]
    return (new_table, new_state)


def flips(value, size):
    table, bit = [value], 1
    while bit < size:
        change = bit - 2 * bit * lax.rem(value // bit, 2)
        table = table + [old + change for old in table]
        bit *= 2
    return table


def ready_groups(chips):
    groups, first = [], 1
    while first < chips:
        size = min(first, READY)
        groups.append(range(first, first + size))
        first += size
    return groups


def exchange_kernel(
    dp, tb, cols, rows, width,
    g_ref, id_ref, state_ref, table_ref, acc, table, state_out,
    pair_g, pair_i, got_g, got_i, part, red, total, full, state,
    send_g, send_i, send_r, send_a, recv_g, recv_i, recv_r, recv_a, own_sem, ready,
):
    d, t = lax.axis_index("dp"), lax.axis_index("table")
    chips = dp * tb // 2
    his = rows // LO
    teams, base = tb // 2, tb // 4
    lines = rows // teams // LANES
    parts = LO // LANES
    each = his // teams
    reducer = jnp.logical_and(t >= base, t < base + teams)
    first_row = d * rows
    ts, ds = flips(t, tb), flips(d, dp)
    core, spot = lax.rem(t, 2), t // 2
    order = t // 4 * (2 * dp) + d * 2 + lax.rem(spot, 2)
    groups = ready_groups(chips)
    sibling = (d, ts[1])
    middle = lax.rem(t // 4 + t // 8, 2) == 1
    far = chips * 3 // 4

    def turns(sequence, near_first):
        sequence = list(sequence)
        close = [group for group in sequence if group[0] < chips // 2]
        cross = [group for group in sequence if chips // 2 <= group[0] < far]
        long = [group for group in sequence if far <= group[0]]
        if near_first:
            first = [(True, group) for group in close]
            return first + [(middle, group) for group in long] + [(True, group) for group in cross] + [
                (jnp.logical_not(middle), group) for group in long
            ]
        last = [(True, group) for group in close]
        return [(middle, group) for group in cross] + [(True, group) for group in long] + [
            (jnp.logical_not(middle), group) for group in cross
        ] + last

    def device(m):
        return ds[m // 2 % dp], ts[m % 2 * 2 + m // (2 * dp) * 4]

    def earlier(group):
        top = 1
        while top * 2 <= group[0]:
            top *= 2
        return lax.rem(order // top, 2) == 1

    def signal(semaphore, to):
        pl.semaphore_signal(semaphore, inc=1, device_id=to, device_id_type=MESH)

    def wait_blocks(ref, sem, count):
        there = ref.at[pl.ds(0, count)]
        pltpu.make_async_copy(there, there, sem).wait()

    barrier = pltpu.get_barrier_semaphore()

    @pl.when(core == 0)
    def _():
        signal(barrier, sibling)

    for group in reversed(groups):
        @pl.when(jnp.logical_not(earlier(group)))
        def _(group=group):
            for m in group:
                signal(barrier, device(m))

    own = (
        pltpu.make_async_copy(g_ref.at[:, core], pair_g.at[:, core], own_sem.at[0]),
        pltpu.make_async_copy(id_ref, pair_i.at[core], own_sem.at[1]),
        pltpu.make_async_copy(state_ref, state, own_sem.at[2]),
        pltpu.make_async_copy(table_ref, table, own_sem.at[3]),
    )
    own[0].start()
    own[1].start()

    @pl.when(order + core > 0)
    def _():
        pl.semaphore_wait(barrier, order + core)

    @pl.when(core == 1)
    def _():
        signal(ready.at[0], sibling)

    for g, group in reversed(list(enumerate(groups))):
        @pl.when(earlier(group))
        def _(g=g, group=group):
            for m in group:
                signal(ready.at[g + 1], device(m))

    @pl.when(core == 0)
    def _():
        pl.semaphore_wait(ready.at[0], 1)

    pltpu.make_async_remote_copy(
        src_ref=id_ref, dst_ref=pair_i.at[core],
        send_sem=send_i.at[0], recv_sem=recv_i.at[0],
        device_id=sibling, device_id_type=MESH,
    ).start()
    pltpu.make_async_remote_copy(
        src_ref=g_ref.at[:, 1 - core], dst_ref=pair_g.at[:, core],
        send_sem=send_g.at[0], recv_sem=recv_g.at[0],
        device_id=sibling, device_id_type=MESH,
    ).start()
    own[2].start()
    own[3].start()
    own[0].wait()
    own[1].wait()
    pltpu.make_async_copy(id_ref, pair_i.at[1 - core], recv_i.at[0]).wait()
    pltpu.make_async_copy(g_ref.at[:, 0], pair_g.at[:, 1 - core], recv_g.at[0]).wait()

    def send(m):
        to = device(m)
        pltpu.make_async_remote_copy(
            src_ref=pair_i, dst_ref=got_i.at[m],
            send_sem=send_i.at[1], recv_sem=recv_i.at[1 + m // GROUP],
            device_id=to, device_id_type=MESH,
        ).start()
        pltpu.make_async_remote_copy(
            src_ref=pair_g.at[to[1] // 2], dst_ref=got_g.at[m],
            send_sem=send_g.at[1], recv_sem=recv_g.at[1 + m // GROUP],
            device_id=to, device_id_type=MESH,
        ).start()

    for turn, group in turns(reversed(groups), False):
        @pl.when(jnp.logical_and(earlier(group), turn))
        def _(group=group):
            for m in reversed(group):
                send(m)

    acc[...] = jnp.zeros_like(acc)
    pltpu.make_async_copy(pair_g.at[spot], got_g.at[0], recv_g.at[1]).start()
    pltpu.make_async_copy(pair_i, got_i.at[0], recv_i.at[1]).start()

    for turn, group in turns(groups, True):
        @pl.when(jnp.logical_and(jnp.logical_not(earlier(group)), turn))
        def _(g=groups.index(group), group=group):
            pl.semaphore_wait(ready.at[g + 1], len(group))
            for m in group:
                send(m)

    def add(sources):
        both = [(m, c) for m in sources for c in range(2)]
        ids = jnp.concatenate([got_i[m, c] for m, c in both], axis=1) - first_row
        grads = jnp.concatenate([got_g[m, c] for m, c in both], axis=1)
        span = ids.shape[1]
        low = jnp.broadcast_to(lax.bitwise_and(ids, LO - 1), (LO, span))
        place = lax.broadcasted_iota(jnp.int32, (LO, span), 0)
        one_hot = jnp.where(low == place, 1.0, 0.0).astype(jnp.bfloat16)
        high = jnp.broadcast_to(lax.shift_right_arithmetic(ids, 8), (cols, span))
        high = jnp.clip(high, -1, his).astype(jnp.float32).astype(jnp.bfloat16)
        zero = jnp.zeros_like(grads)
        picked = jnp.concatenate(
            [jnp.where(high == jnp.bfloat16(h), grads, zero) for h in range(his)], axis=0
        )
        acc[...] += lax.dot_general(
            picked, one_hot, (((1,), (1,)), ((), ())), preferred_element_type=jnp.float32
        )

    @pl.loop(0, chips // GROUP)
    def _(turn):
        half = chips // GROUP // 2
        quarter = chips // GROUP // 4
        swap = jnp.where(jnp.logical_and(middle, turn >= half), 1, 0)
        g = turn + swap * (quarter - 2 * quarter * ((turn - half) // quarter))
        wait_blocks(got_i, recv_i.at[1 + g], GROUP)
        wait_blocks(got_g, recv_g.at[1 + g], GROUP)
        add([g * GROUP + m for m in range(GROUP)])

    planes = teams // 4
    upper = t // (tb // 2)

    def plane(r):
        return planes - 1 - r + upper * (2 * r - planes + 1)

    slots = [(r, low) for r in range(planes) for low in reversed(range(4))]

    def team_of(slot):
        r, low = slots[slot]
        return plane(r) * 4 + lax.rem(ts[low], 4)

    def send_part(slot):
        team = team_of(slot)

        @pl.when(team + base != t)
        def _():
            pltpu.make_async_remote_copy(
                src_ref=part.at[slot], dst_ref=red.at[t],
                send_sem=send_r.at[0], recv_sem=recv_r.at[0],
                device_id=(d, team + base), device_id_type=MESH,
            ).start()

    def square(slot):
        pieces = []
        for h in range(each):
            at = pl.multiple_of((team_of(slot) * each + h) * cols, cols)
            piece = acc[pl.ds(at, cols), :]
            sums = jnp.sum(piece * piece, axis=0, keepdims=True)
            for half in range(parts):
                pieces.append(sums[:, half * LANES:(half + 1) * LANES])
        part[slot] = jnp.concatenate(pieces, axis=0)

    for first in range(0, teams, 4):
        for slot in range(first, first + 4):
            square(slot)
        for slot in range(first, first + 4):
            send_part(slot)

    own[2].wait()

    @pl.when(reducer)
    def _():
        mine = t - base
        red[t] = part[teams - 1]
        wait_blocks(red, recv_r.at[0], tb - 1)
        here = pl.ds(pl.multiple_of(mine * lines, lines), lines)
        fresh = state[here, :] + jnp.sum(red[...], axis=0) / width
        total[...] = fresh
        full[mine] = fresh
        near = tb // 4
        for k in [*range(2 * near, 3 * near), *range(near, 2 * near), *range(3 * near, tb), *range(1, near)]:
            pltpu.make_async_remote_copy(
                src_ref=total, dst_ref=full.at[mine],
                send_sem=send_a.at[0], recv_sem=recv_a.at[0],
                device_id=(d, ts[k]), device_id_type=MESH,
            ).start()

    own[3].wait()
    pltpu.make_async_copy(g_ref.at[:, 0], pair_g.at[:, 0], send_g.at[0]).wait()
    pltpu.make_async_copy(id_ref, pair_i.at[0], send_i.at[0]).wait()
    wait_blocks(got_g, send_g.at[1], chips - 1)
    wait_blocks(got_i, send_i.at[1], chips - 1)

    @pl.when(reducer)
    def _():
        wait_blocks(red, send_r.at[0], teams - 1)
        wait_blocks(full, recv_a.at[0], teams - 1)
        wait_blocks(red, send_a.at[0], tb - 1)

    @pl.when(jnp.logical_not(reducer))
    def _():
        wait_blocks(red, send_r.at[0], teams)
        wait_blocks(full, recv_a.at[0], teams)

    state_out[...] = full[...]


def finish_kernel(acc, table, state, table_out, state_out, fresh_table, sems):
    teams, lines, _ = state.shape
    cols, rows = table.shape
    parts = LO // LANES
    each = lines // parts
    size = rows // PIECES
    copies = [pltpu.make_async_copy(state, state_out, sems.at[PIECES])]
    copies[0].start()
    for p in range(PIECES):
        for j in range(p * teams // PIECES, (p + 1) * teams // PIECES):
            scale = learn_rate / jnp.sqrt(state[j])
            for r in range(lines):
                at, half = (j * each + r // parts) * cols, r % parts
                lanes = slice((j * lines + r) * LANES, (j * lines + r + 1) * LANES)
                step = acc[at:at + cols, half * LANES:(half + 1) * LANES]
                fresh_table[:, lanes] = table[:, lanes] - step * scale[r:r + 1, :]
        there = pl.ds(p * size, size)
        copies.append(pltpu.make_async_copy(fresh_table.at[:, there], table_out.at[:, there], sems.at[p]))
        copies[-1].start()
    for copy in copies:
        copy.wait()


def kernel_body(dp, tb, width, gradients, row_ids, table_block, adagrad_state):
    cols, rows = table_block.shape
    count = row_ids.shape[0]
    chips = dp * tb // 2
    his = rows // LO
    teams = tb // 2
    lines = rows // teams // LANES
    dma = pltpu.SemaphoreType.DMA
    row_grad, table, state = pl.pallas_call(
        functools.partial(exchange_kernel, dp, tb, cols, rows, width),
        name="exchange",
        out_shape=(
            pltpu.VMEM((his * cols, LO), jnp.float32),
            pltpu.VMEM((cols, rows), jnp.float32),
            pltpu.VMEM((teams, lines, LANES), jnp.float32),
        ),
        in_specs=[pl.BlockSpec(memory_space=pl.ANY)] * 4,
        out_specs=(pl.BlockSpec(memory_space=pltpu.VMEM),) * 3,
        scratch_shapes=[
            pltpu.VMEM((tb // 2, 2, cols, count), jnp.bfloat16),
            pltpu.VMEM((2, 1, count), jnp.int32),
            pltpu.VMEM((chips, 2, cols, count), jnp.bfloat16),
            pltpu.VMEM((chips, 2, 1, count), jnp.int32),
            pltpu.VMEM((teams, lines, LANES), jnp.float32),
            pltpu.VMEM((tb, lines, LANES), jnp.float32),
            pltpu.VMEM((lines, LANES), jnp.float32),
            pltpu.VMEM((teams, lines, LANES), jnp.float32),
            pltpu.VMEM((rows // LANES, LANES), jnp.float32),
            dma((2,)), dma((2,)), dma((1,)), dma((1,)),
            dma((1 + chips // GROUP,)), dma((1 + chips // GROUP,)), dma((1,)), dma((1,)),
            dma((4,)),
            pltpu.SemaphoreType.REGULAR((1 + len(ready_groups(chips)),)),
        ],
        compiler_params=pltpu.CompilerParams(collective_id=0, has_side_effects=True),
    )(
        gradients.reshape(tb // 2, 2, cols, count),
        row_ids.reshape(1, count),
        adagrad_state.reshape(rows // LANES, LANES),
        table_block,
    )
    new_table, new_state = pl.pallas_call(
        finish_kernel,
        name="finish",
        out_shape=(
            jax.ShapeDtypeStruct((cols, rows), jnp.float32),
            jax.ShapeDtypeStruct((teams, lines, LANES), jnp.float32),
        ),
        in_specs=[pl.BlockSpec(memory_space=pltpu.VMEM)] * 3,
        out_specs=(pl.BlockSpec(memory_space=pl.ANY),) * 2,
        scratch_shapes=[pltpu.VMEM((cols, rows), jnp.float32), dma((PIECES + 1,))],
    )(
        pltpu.with_memory_space_constraint(row_grad, pltpu.VMEM),
        pltpu.with_memory_space_constraint(table, pltpu.VMEM),
        pltpu.with_memory_space_constraint(state, pltpu.VMEM),
    )
    return (new_table, new_state.reshape(rows))


def body(dp, tb, gradients, row_ids, table_block, adagrad_state):
    width = gradients.shape[0]
    cols, rows = table_block.shape
    fits = (
        cols % 16 == 0
        and rows % (tb * 8 * LANES) == 0
        and rows % (4 * LO * 4) == 0
        and dp & (dp - 1) == 0
        and tb & (tb - 1) == 0
        and tb % 16 == 0
        and dp * tb % (8 * GROUP) == 0
        and rows // LO <= 256
        and row_ids.shape[0] == LANES
    )
    args = (gradients, row_ids, table_block, adagrad_state)
    if fits:
        return kernel_body(dp, tb, width, *args)
    return plain_body(width, *args)


def solution(mesh):
    in_specs = (P(None, ("dp", "table")), P(("dp", "table")), P("table", "dp"), P("dp"))
    out_specs = (P("table", "dp"), P("dp"))
    run = functools.partial(body, mesh.shape["dp"], mesh.shape["table"])
    return jax.shard_map(run, mesh=mesh, in_specs=in_specs, out_specs=out_specs, check_vma=False)
```
